32 devices in a mesh: wide: 8 (over z, core), sub: 4 (over y, x).
Axes of the slice: x: 2, y: 2, z: 4, core: 2. Of those that a mesh axis runs over, the one named last changes fastest.
Arguments:
- passages: bfloat16 [64, 1024], P('sub'), may hold values from -6 to 6
- enc_weight: bfloat16 [1024, 16384], P(None, ('wide', 'sub')), may hold values from -0.1875 to 0.1875
- enc_bias: float32 [16384], P(('wide', 'sub')), may hold values from -4 to 4
- dec_weight: bfloat16 [16384, 1024], P(('wide', 'sub')), may hold values from -0.09375 to 0.09375
- dec_bias: float32 [1024], replicated, may hold values from -4 to 4
- active: int32 [64, 16384], P(None, ('wide', 'sub')), may hold values 0 or 1
Outputs:
- grad_enc: bfloat16 [1024, 16384], P(None, ('wide', 'sub'))
- grad_enc_bias: float32 [16384], P(('wide', 'sub'))
- grad_dec: bfloat16 [16384, 1024], P(('wide', 'sub'))
- grad_dec_bias: float32 [1024], replicated
- grad_input: float32 [64, 1024], P('sub')
The draws below stay inside these ranges and needn't reach their ends.
All inputs are finite; a program needn't handle non-finite values. No bound on the sum of `active` on one device may be relied on, other than what follows from the above.
Results may differ from the reference program's by a relative error of at most 0.014.
Values may be sent and summed in bfloat16 or wider, within the bound.
No kernel may reach another device: no remote copies, remote signals or barrier semaphores. Data moves between devices by JAX's collectives and lax.ppermute only.
A program may use at most 64 MiB of HBM per device.

```python
import jax
import jax.numpy as jnp

D = 1024
LATENTS = 16384
ROWS = 64


def plant(values, rng, least, largest):
    shape = values.shape
    spot = [jax.random.randint(jax.random.fold_in(rng, axis), (), 0, shape[axis]) for axis in range(len(shape))]
    values = values.at[tuple(spot)].set(least)
    longest = shape.index(max(shape))
    spot[longest] = (spot[longest] + 1) % shape[longest]
    return values.at[tuple(spot)].set(largest)


def block_scale(key, dims, cuts, low, largest):
    def one(dim, shards_of):
        steps = jax.random.uniform(jax.random.fold_in(jax.random.fold_in(key, 6), dim), (shards_of,), jnp.float32, low / len(cuts), largest / len(cuts))
        return jnp.repeat(jnp.exp(steps), dims[dim] // shards_of).reshape((-1,) + (1,) * (len(dims) - dim - 1))

    level = one(*cuts[0])
    for cut in cuts[1:]:
        level = level * one(*cut)
    return level


def noise(own_key, shape, spread, reach, shards=(), held_as=jnp.bfloat16):
    array = spread * jax.random.normal(own_key, shape, jnp.float32)
    if shards:
        array = array * block_scale(own_key, shape, shards, -0.22, 0.18)
    return jnp.clip(array, -reach, reach).astype(held_as)


def setup_inputs(seed: int = 0) -> dict:
    streams_of = jax.random.split(jax.random.key(seed), 7)
    return {
        "passages": noise(streams_of[0], (ROWS, D), 1.0, 6.0, ((0, 4),)),
        "enc_weight": noise(streams_of[1], (D, LATENTS), D ** -0.5, 0.1875, ((1, 32),)),
        "enc_bias": noise(streams_of[2], (LATENTS,), 0.7, 4.0, ((0, 32),), jnp.float32),
        "dec_weight": noise(streams_of[3], (LATENTS, D), (LATENTS // 4) ** -0.5, 0.09375, ((0, 32),)),
        "dec_bias": noise(streams_of[4], (D,), 0.7, 4.0, (), jnp.float32),
        "active": plant((jax.random.randint(streams_of[5], (ROWS, LATENTS), 0, 4) < 1).astype(jnp.int32), jax.random.fold_in(streams_of[5], 1), 0, 1),
    }


def reference(passages, enc_weight, enc_bias, dec_weight, dec_bias, active):
    gate = active.astype(jnp.float32)
    pre = jnp.dot(passages, enc_weight, preferred_element_type=jnp.float32) + enc_bias
    codes = (gate * pre).astype(jnp.bfloat16)
    recon = jnp.dot(codes, dec_weight, preferred_element_type=jnp.float32) + dec_bias
    resid = (recon - passages.astype(jnp.float32)).astype(jnp.bfloat16)
    grad_dec = jnp.dot(codes.T, resid, preferred_element_type=jnp.float32).astype(jnp.bfloat16)
    grad_dec_bias = jnp.sum(resid.astype(jnp.float32), axis=0)
    back = jnp.dot(resid, dec_weight.T, preferred_element_type=jnp.float32)
    dpre = (gate * back).astype(jnp.bfloat16)
    grad_enc = jnp.dot(passages.T, dpre, preferred_element_type=jnp.float32).astype(jnp.bfloat16)
    grad_enc_bias = jnp.sum(dpre.astype(jnp.float32), axis=0)
    grad_input = jnp.dot(dpre, enc_weight.T, preferred_element_type=jnp.float32) - resid.astype(jnp.float32)
    return grad_enc, grad_enc_bias, grad_dec, grad_dec_bias, grad_input
```

```python
import jax
import jax.numpy as jnp
from jax import lax
from jax.sharding import PartitionSpec as P

AXES = ("wide", "sub")


def swap(x, size, mask):
    return lax.ppermute(x, AXES, [(i, i ^ mask) for i in range(size)])


def crossing(mask, core):
    return mask ^ core if mask.bit_count() % 2 else mask


def make_per_device(wide, sub):
    size = wide * sub
    core = sub
    sub_bits = [b for b in (1 << k for k in range(sub.bit_length())) if b < sub]
    z_bits = [b for b in (1 << k for k in range(size.bit_length())) if 2 * sub <= b < size]

    def rounds(bits):
        out = []
        for k in range(0, len(bits), 2):
            pair = bits[k : k + 2]
            out.append(pair if len(pair) == 1 else [pair[0], pair[1], pair[0] ^ pair[1]])
        return out

    def total(parts):
        parts = [p.astype(jnp.float32) for p in parts]
        while len(parts) > 1:
            parts = [parts[k] + parts[k + 1] for k in range(0, len(parts), 2)]
        return parts[0]

    def sum_over(x, bits, order=lambda got, mask: got):
        for masks in rounds(bits):
            got = [swap(x, size, crossing(m, core)) for m in masks]
            x = total([x] + [order(g, m) for g, m in zip(got, masks)])
            yield_last = x
            x = x.astype(jnp.bfloat16)
        return yield_last

    def per_device(passages, enc_weight, enc_bias, dec_weight, dec_bias, active):
        rows, width = passages.shape
        half = width // 2
        me = lax.axis_index(AXES)
        mine = lax.axis_index("sub")
        odd = me
        for k in (16, 8, 4, 2, 1):
            odd = odd ^ (odd >> k)
        high = (odd & 1) == 1

        blocks = [passages] + [swap(passages, size, crossing(k, core)) for k in range(1, sub)]
        every = jnp.concatenate(blocks, axis=0)
        gate = jnp.concatenate(
            [lax.dynamic_slice_in_dim(active, (mine ^ k) * rows, rows, 0) for k in range(sub)], axis=0
        ).astype(jnp.float32)

        def pick(x):
            keep = jnp.where(high, x[:, half:], x[:, :half])
            send = jnp.where(high, x[:, :half], x[:, half:])
            return keep, send.astype(jnp.bfloat16)

        def join(own, other):
            left = jnp.where(high, other, own)
            right = jnp.where(high, own, other)
            return jnp.concatenate([left, right], axis=1)

        def reorder(got, mask):
            parts = [got[(k ^ mask) * rows : ((k ^ mask) + 1) * rows] for k in range(sub)]
            return jnp.concatenate(parts, axis=0)

        pre = jnp.dot(every, enc_weight, preferred_element_type=jnp.float32) + enc_bias
        codes = (gate * pre).astype(jnp.bfloat16)
        part = jnp.dot(codes, dec_weight, preferred_element_type=jnp.float32)
        keep, send = pick(part)
        x = (keep + swap(send, size, core).astype(jnp.float32)).astype(jnp.bfloat16)
        x = sum_over(x, sub_bits, reorder).astype(jnp.bfloat16)
        recon = sum_over(x, z_bits)
        base = dec_bias - every.astype(jnp.float32)
        own = (recon + jnp.where(high, base[:, half:], base[:, :half])).astype(jnp.bfloat16)
        resid = join(own, swap(own, size, core))

        back = lax.dot_general(
            resid, dec_weight, (((1,), (1,)), ((), ())), preferred_element_type=jnp.float32
        )
        dpre = (gate * back).astype(jnp.bfloat16)
        grad = lax.dot_general(
            dpre, enc_weight, (((1,), (1,)), ((), ())), preferred_element_type=jnp.float32
        )
        keep, send = pick(grad)
        x = keep + swap(send, size, core).astype(jnp.float32)
        x = x.astype(jnp.bfloat16)
        got = [swap(x[k * rows : (k + 1) * rows], size, crossing(k, core)) for k in range(1, sub)]
        x = total([x[:rows]] + got).astype(jnp.bfloat16)
        own = sum_over(x, z_bits).astype(jnp.bfloat16)
        summed = join(own, swap(own, size, core))
        grad_input = summed.astype(jnp.float32) - resid[:rows].astype(jnp.float32)

        grad_dec = lax.dot_general(
            codes, resid, (((0,), (0,)), ((), ())), preferred_element_type=jnp.float32
        ).astype(jnp.bfloat16)
        grad_dec_bias = jnp.sum(resid.astype(jnp.float32), axis=0)
        grad_enc = lax.dot_general(
            every, dpre, (((0,), (0,)), ((), ())), preferred_element_type=jnp.float32
        ).astype(jnp.bfloat16)
        grad_enc_bias = jnp.sum(dpre.astype(jnp.float32), axis=0)
        return (grad_enc, grad_enc_bias, grad_dec, grad_dec_bias, grad_input)

    return per_device


def solution(mesh):
    in_specs = (
        P("sub", None),
        P(None, ("wide", "sub")),
        P(("wide", "sub")),
        P(("wide", "sub"), None),
        P(),
        P(None, ("wide", "sub")),
    )
    out_specs = (
        P(None, ("wide", "sub")),
        P(("wide", "sub")),
        P(("wide", "sub"), None),
        P(),
        P("sub", None),
    )
    per_device = make_per_device(mesh.shape["wide"], mesh.shape["sub"])
    return jax.shard_map(
        per_device, mesh=mesh, in_specs=in_specs, out_specs=out_specs, check_vma=False
    )
```

```python
import jax
import jax.numpy as jnp
from jax import lax
from jax.sharding import PartitionSpec as P


AXES = ("wide", "sub")


def swap(x, size, mask):
    return lax.ppermute(x, AXES, [(i, i ^ mask) for i in range(size)])


def crossing(mask, core):
    return mask ^ core if mask.bit_count() % 2 else mask


def make_per_device(wide, sub):
    size = wide * sub
    core = sub
    sub_bits = [b for b in (1 << k for k in range(sub.bit_length())) if b < sub]
    z_bits = [b for b in (1 << k for k in range(size.bit_length())) if 2 * sub <= b < size]

    def rounds(bits):
        out = []
        for k in range(0, len(bits), 2):
            pair = bits[k : k + 2]
            out.append(pair if len(pair) == 1 else [pair[0], pair[1], pair[0] ^ pair[1]])
        return out

    def total(parts):
        parts = [p.astype(jnp.float32) for p in parts]
        while len(parts) > 1:
            parts = [parts[k] + parts[k + 1] for k in range(0, len(parts), 2)]
        return parts[0]

    def sum_over(x, bits, order=lambda got, mask: got):
        for masks in rounds(bits):
            got = [swap(x, size, crossing(m, core)) for m in masks]
            exact = total([x] + [order(g, m) for g, m in zip(got, masks)])
            x = exact.astype(jnp.bfloat16)
        return exact

    def per_device(passages, enc_weight, enc_bias, dec_weight, dec_bias, active):
        rows, width = passages.shape
        half = width // 2
        me = lax.axis_index(AXES)
        mine = lax.axis_index("sub")
        odd = me
        for k in (16, 8, 4, 2, 1):
            odd = odd ^ (odd >> k)
        high = (odd & 1) == 1

        blocks = [passages] + [swap(passages, size, crossing(k, core)) for k in range(1, sub)]
        every = jnp.concatenate(blocks, axis=0)
        gate = jnp.concatenate(
            [lax.dynamic_slice_in_dim(active, (mine ^ k) * rows, rows, 0) for k in range(sub)], axis=0
        ).astype(jnp.float32)

        def pick(x):
            keep = jnp.where(high, x[:, half:], x[:, :half])
            send = jnp.where(high, x[:, :half], x[:, half:])
            return keep, send.astype(jnp.bfloat16)

        def join(own, other):
            left = jnp.where(high, other, own)
            right = jnp.where(high, own, other)
            return jnp.concatenate([left, right], axis=1)

        def reorder(got, mask):
            parts = [got[(k ^ mask) * rows : ((k ^ mask) + 1) * rows] for k in range(sub)]
            return jnp.concatenate(parts, axis=0)

        pre = jnp.concatenate(
            [
                jnp.dot(passages, enc_weight, preferred_element_type=jnp.float32),
                jnp.dot(every[rows:], enc_weight, preferred_element_type=jnp.float32),
            ],
            axis=0,
        )
        pre = pre + enc_bias
        codes = (gate * pre).astype(jnp.bfloat16)
        part = jnp.dot(codes, dec_weight, preferred_element_type=jnp.float32)
        keep, send = pick(part)
        x = (keep + swap(send, size, core).astype(jnp.float32)).astype(jnp.bfloat16)
        x = sum_over(x, sub_bits, reorder).astype(jnp.bfloat16)
        recon = sum_over(x, z_bits)
        base = dec_bias - every.astype(jnp.float32)
        own = (recon + jnp.where(high, base[:, half:], base[:, :half])).astype(jnp.bfloat16)
        resid = join(own, swap(own, size, core))

        back = lax.dot_general(
            resid, dec_weight, (((1,), (1,)), ((), ())), preferred_element_type=jnp.float32
        )
        dpre = (gate * back).astype(jnp.bfloat16)
        grad = lax.dot_general(
            dpre, enc_weight, (((1,), (1,)), ((), ())), preferred_element_type=jnp.float32
        )
        keep, send = pick(grad)
        x = keep + swap(send, size, core).astype(jnp.float32)
        x = x.astype(jnp.bfloat16)
        grad_dec = lax.dot_general(
            codes, resid, (((0,), (0,)), ((), ())), preferred_element_type=jnp.float32
        ).astype(jnp.bfloat16)
        grad_enc = lax.dot_general(
            every, dpre, (((0,), (0,)), ((), ())), preferred_element_type=jnp.float32
        ).astype(jnp.bfloat16)
        grad_dec_bias = jnp.sum(lax.optimization_barrier(resid).astype(jnp.float32), axis=0)
        grad_enc_bias = jnp.sum(lax.optimization_barrier(dpre).astype(jnp.float32), axis=0)

        got = [swap(x[k * rows : (k + 1) * rows], size, crossing(k, core)) for k in range(1, sub)]
        x = total([x[:rows]] + got).astype(jnp.bfloat16)
        own = sum_over(x, z_bits).astype(jnp.bfloat16)
        summed = join(own, swap(own, size, core))
        grad_input = summed.astype(jnp.float32) - resid[:rows].astype(jnp.float32)
        return (grad_enc, grad_enc_bias, grad_dec, grad_dec_bias, grad_input)

    return per_device


def solution(mesh):
    in_specs = (
        P("sub", None),
        P(None, ("wide", "sub")),
        P(("wide", "sub")),
        P(("wide", "sub"), None),
        P(),
        P(None, ("wide", "sub")),
    )
    out_specs = (
        P(None, ("wide", "sub")),
        P(("wide", "sub")),
        P(("wide", "sub"), None),
        P(),
        P("sub", None),
    )
    per_device = make_per_device(mesh.shape["wide"], mesh.shape["sub"])

    return jax.shard_map(
        per_device, mesh=mesh, in_specs=in_specs, out_specs=out_specs, check_vma=False
    )
```

```python
import jax
import jax.numpy as jnp
from jax import lax
from jax.sharding import PartitionSpec as P


AXES = ("wide", "sub")


def swap(x, size, mask):
    return lax.ppermute(x, AXES, [(i, i ^ mask) for i in range(size)])


CROSS = 0b11011
OWN = 0b1110
LAST = 0b1110
FIRST = 0b1100


def crossing(mask, core):
    return mask ^ core if (mask & CROSS).bit_count() % 2 else mask


def make_per_device(wide, sub):
    size = wide * sub
    core = sub
    sub_bits = [b for b in (1 << k for k in range(sub.bit_length())) if b < sub]
    z_bits = [b for b in (1 << k for k in range(size.bit_length())) if 2 * sub <= b < size]

    def rounds(bits):
        out = []
        for k in range(0, len(bits), 2):
            pair = bits[k : k + 2]
            out.append(pair if len(pair) == 1 else [pair[0], pair[1], pair[0] ^ pair[1]])
        return out

    def total(parts):
        parts = [p.astype(jnp.float32) for p in parts]
        while len(parts) > 1:
            parts = [parts[k] + parts[k + 1] for k in range(0, len(parts), 2)]
        return parts[0]

    def sum_over(x, bits, order=lambda got, mask: got, cross=None):
        for masks in rounds(bits):
            got = [
                swap(x, size, crossing(m, core) if cross is None else m ^ (core if cross >> (k + 1) & 1 else 0))
                for k, m in enumerate(masks)
            ]
            exact = total([x] + [order(g, m) for g, m in zip(got, masks)])
            x = exact.astype(jnp.bfloat16)
        return exact

    def per_device(passages, enc_weight, enc_bias, dec_weight, dec_bias, active):
        rows, width = passages.shape
        half = width // 2
        me = lax.axis_index(AXES)
        mine = lax.axis_index("sub")
        odd = me & (CROSS | core)
        for k in (16, 8, 4, 2, 1):
            odd = odd ^ (odd >> k)
        high = (odd & 1) == 1

        blocks = [passages] + [swap(passages, size, k ^ (core if FIRST >> k & 1 else 0)) for k in range(1, sub)]
        every = jnp.concatenate(blocks, axis=0)
        gate = jnp.concatenate(
            [lax.dynamic_slice_in_dim(active, (mine ^ k) * rows, rows, 0) for k in range(sub)], axis=0
        ).astype(jnp.float32)

        def join(own, other):
            left = jnp.where(high, other, own)
            right = jnp.where(high, own, other)
            return jnp.concatenate([left, right], axis=1)

        def reorder(got, mask):
            parts = [got[(k ^ mask) * rows : ((k ^ mask) + 1) * rows] for k in range(sub)]
            return jnp.concatenate(parts, axis=0)

        pre = jnp.concatenate(
            [
                jnp.dot(passages, enc_weight, preferred_element_type=jnp.float32),
                jnp.dot(every[rows:], enc_weight, preferred_element_type=jnp.float32),
            ],
            axis=0,
        )
        pre = pre + enc_bias
        codes = (gate * pre).astype(jnp.bfloat16)
        mine_at = jnp.where(high, half, 0)
        send = jnp.dot(
            codes,
            lax.dynamic_slice_in_dim(dec_weight, half - mine_at, half, 1),
            preferred_element_type=jnp.float32,
        ).astype(jnp.bfloat16)
        got = swap(send, size, core)
        keep = jnp.dot(
            codes,
            lax.dynamic_slice_in_dim(dec_weight, mine_at, half, 1),
            preferred_element_type=jnp.float32,
        )
        x = (lax.optimization_barrier(keep) + got.astype(jnp.float32)).astype(jnp.bfloat16)
        x = sum_over(x, sub_bits, reorder).astype(jnp.bfloat16)
        recon = sum_over(x, z_bits)
        base = dec_bias - every.astype(jnp.float32)
        own = (recon + jnp.where(high, base[:, half:], base[:, :half])).astype(jnp.bfloat16)
        other = swap(own, size, core)
        resid = join(own, other)
        mine_at = jnp.where(high, half, 0)

        def against(part, at):
            return lax.dot_general(
                part,
                lax.dynamic_slice_in_dim(dec_weight, at, half, 1),
                (((1,), (1,)), ((), ())),
                preferred_element_type=jnp.float32,
            )

        back = lax.optimization_barrier(against(own, mine_at))
        back = back + against(other, half - mine_at)
        dpre = (gate * back).astype(jnp.bfloat16)
        grad = lax.dot_general(
            dpre, enc_weight, (((1,), (1,)), ((), ())), preferred_element_type=jnp.float32
        )
        grad = grad.astype(jnp.bfloat16)
        x = (grad.astype(jnp.float32) + swap(grad, size, core).astype(jnp.float32)).astype(jnp.bfloat16)
        grad_dec = lax.dot_general(
            codes, resid, (((0,), (0,)), ((), ())), preferred_element_type=jnp.float32
        ).astype(jnp.bfloat16)
        grad_enc = lax.dot_general(
            every, dpre, (((0,), (0,)), ((), ())), preferred_element_type=jnp.float32
        ).astype(jnp.bfloat16)
        grad_dec_bias = jnp.sum(lax.optimization_barrier(resid).astype(jnp.float32), axis=0)
        grad_enc_bias = jnp.sum(lax.optimization_barrier(dpre).astype(jnp.float32), axis=0)

        got = [swap(x[k * rows : (k + 1) * rows], size, k ^ (core if OWN >> k & 1 else 0)) for k in range(1, sub)]
        x = total([x[:rows]] + got).astype(jnp.bfloat16)
        grad_input = sum_over(x, z_bits, cross=LAST) - resid[:rows].astype(jnp.float32)
        return (grad_enc, grad_enc_bias, grad_dec, grad_dec_bias, grad_input)

    return per_device


def solution(mesh):
    in_specs = (
        P("sub", None),
        P(None, ("wide", "sub")),
        P(("wide", "sub")),
        P(("wide", "sub"), None),
        P(),
        P(None, ("wide", "sub")),
    )
    out_specs = (
        P(None, ("wide", "sub")),
        P(("wide", "sub")),
        P(("wide", "sub"), None),
        P(),
        P("sub", None),
    )
    per_device = make_per_device(mesh.shape["wide"], mesh.shape["sub"])

    return jax.shard_map(per_device, mesh=mesh, in_specs=in_specs, out_specs=out_specs, check_vma=False)
```

```python
import jax
import jax.numpy as jnp
from jax import lax
from jax.sharding import PartitionSpec as P


AXES = ("wide", "sub")


def swap(x, size, mask):
    return lax.ppermute(x, AXES, [(i, i ^ mask) for i in range(size)])


CROSS = 0b11011
OWN = 0b1110
LAST = 0b1110
FIRST = 0b1100


def crossing(mask, core):
    return mask ^ core if (mask & CROSS).bit_count() % 2 else mask


def make_per_device(wide, sub):
    size = wide * sub
    core = sub
    sub_bits = [b for b in (1 << k for k in range(sub.bit_length())) if b < sub]
    z_bits = [b for b in (1 << k for k in range(size.bit_length())) if 2 * sub <= b < size]

    def rounds(bits):
        out = []
        for k in range(0, len(bits), 2):
            pair = bits[k : k + 2]
            out.append(pair if len(pair) == 1 else [pair[0], pair[1], pair[0] ^ pair[1]])
        return out

    def total(parts):
        parts = [p.astype(jnp.float32) for p in parts]
        while len(parts) > 1:
            parts = [parts[k] + parts[k + 1] for k in range(0, len(parts), 2)]
        return parts[0]

    def sum_over(x, bits, order=lambda got, mask: got, cross=None):
        for masks in rounds(bits):
            got = [
                swap(x, size, crossing(m, core) if cross is None else m ^ (core if cross >> (k + 1) & 1 else 0))
                for k, m in enumerate(masks)
            ]
            exact = total([x] + [order(g, m) for g, m in zip(got, masks)])
            x = exact.astype(jnp.bfloat16)
        return exact

    def per_device(passages, enc_weight, enc_bias, dec_weight, dec_bias, active):
        rows, width = passages.shape
        half = width // 2
        me = lax.axis_index(AXES)
        mine = lax.axis_index("sub")
        odd = me & (CROSS | core)
        for k in (16, 8, 4, 2, 1):
            odd = odd ^ (odd >> k)
        high = (odd & 1) == 1

        blocks = [passages] + [swap(passages, size, k ^ (core if FIRST >> k & 1 else 0)) for k in range(1, sub)]
        every = jnp.concatenate(blocks, axis=0)
        gate = jnp.concatenate(
            [lax.dynamic_slice_in_dim(active, (mine ^ k) * rows, rows, 0) for k in range(sub)], axis=0
        ).astype(jnp.float32)

        def join(own, other):
            left = jnp.where(high, other, own)
            right = jnp.where(high, own, other)
            return jnp.concatenate([left, right], axis=1)

        def reorder(got, mask):
            parts = [got[(k ^ mask) * rows : ((k ^ mask) + 1) * rows] for k in range(sub)]
            return jnp.concatenate(parts, axis=0)

        pre = jnp.concatenate(
            [
                jnp.dot(passages, enc_weight, preferred_element_type=jnp.float32),
                jnp.dot(every[rows:], enc_weight, preferred_element_type=jnp.float32),
            ],
            axis=0,
        )
        pre = pre + enc_bias
        codes = (gate * pre).astype(jnp.bfloat16)
        mine_at = jnp.where(high, half, 0)
        send = jnp.dot(
            codes,
            lax.dynamic_slice_in_dim(dec_weight, half - mine_at, half, 1),
            preferred_element_type=jnp.float32,
        ).astype(jnp.bfloat16)
        got = swap(send, size, core)
        keep = jnp.dot(
            codes,
            lax.dynamic_slice_in_dim(dec_weight, mine_at, half, 1),
            preferred_element_type=jnp.float32,
        )
        x = (lax.optimization_barrier(keep) + got.astype(jnp.float32)).astype(jnp.bfloat16)
        x = sum_over(x, sub_bits, reorder).astype(jnp.bfloat16)
        recon = sum_over(x, z_bits)
        base = dec_bias - every.astype(jnp.float32)
        own = (recon + jnp.where(high, base[:, half:], base[:, :half])).astype(jnp.bfloat16)
        other = swap(own, size, core)
        resid = join(own, other)
        mine_at = jnp.where(high, half, 0)

        def against(part, at):
            return lax.dot_general(
                part,
                lax.dynamic_slice_in_dim(dec_weight, at, half, 1),
                (((1,), (1,)), ((), ())),
                preferred_element_type=jnp.float32,
            )

        back = lax.optimization_barrier(against(own, mine_at))
        back = back + against(other, half - mine_at)
        dpre = (gate * back).astype(jnp.bfloat16)
        dpre_other = swap(dpre, size, core)
        weight = swap(enc_weight, size, core)

        def spread(part, by):
            return lax.dot_general(
                part, by, (((1,), (1,)), ((), ())), preferred_element_type=jnp.float32
            )

        grad = lax.optimization_barrier(spread(dpre, enc_weight))
        x = (grad + spread(dpre_other, weight)).astype(jnp.bfloat16)
        grad_dec = lax.dot_general(
            codes, resid, (((0,), (0,)), ((), ())), preferred_element_type=jnp.float32
        ).astype(jnp.bfloat16)
        grad_enc = lax.dot_general(
            every, dpre, (((0,), (0,)), ((), ())), preferred_element_type=jnp.float32
        ).astype(jnp.bfloat16)
        grad_dec_bias = jnp.sum(lax.optimization_barrier(resid).astype(jnp.float32), axis=0)
        grad_enc_bias = jnp.sum(lax.optimization_barrier(dpre).astype(jnp.float32), axis=0)

        got = [swap(x[k * rows : (k + 1) * rows], size, k ^ (core if OWN >> k & 1 else 0)) for k in range(1, sub)]
        x = total([x[:rows]] + got).astype(jnp.bfloat16)
        grad_input = sum_over(x, z_bits, cross=LAST) - resid[:rows].astype(jnp.float32)
        return (grad_enc, grad_enc_bias, grad_dec, grad_dec_bias, grad_input)

    return per_device


def solution(mesh):
    in_specs = (
        P("sub", None),
        P(None, ("wide", "sub")),
        P(("wide", "sub")),
        P(("wide", "sub"), None),
        P(),
        P(None, ("wide", "sub")),
    )
    out_specs = (
        P(None, ("wide", "sub")),
        P(("wide", "sub")),
        P(("wide", "sub"), None),
        P(),
        P("sub", None),
    )
    per_device = make_per_device(mesh.shape["wide"], mesh.shape["sub"])

    return jax.shard_map(per_device, mesh=mesh, in_specs=in_specs, out_specs=out_specs, check_vma=False)
```

```python
import jax
import jax.numpy as jnp
from jax import lax
from jax.sharding import PartitionSpec as P


AXES = ("wide", "sub")


def swap(x, size, mask):
    return lax.ppermute(x, AXES, [(i, i ^ mask) for i in range(size)])


CROSS = 0b11011
OWN = 0b1110
LAST = 0b1110
FIRST = 0b1100


def crossing(mask, core):
    return mask ^ core if (mask & CROSS).bit_count() % 2 else mask


def make_per_device(wide, sub):
    size = wide * sub
    core = sub
    sub_bits = [b for b in (1 << k for k in range(sub.bit_length())) if b < sub]
    z_bits = [b for b in (1 << k for k in range(size.bit_length())) if 2 * sub <= b < size]

    def rounds(bits):
        out = []
        for k in range(0, len(bits), 2):
            pair = bits[k : k + 2]
            out.append(pair if len(pair) == 1 else [pair[0], pair[1], pair[0] ^ pair[1]])
        return out

    def total(parts):
        parts = [p.astype(jnp.float32) for p in parts]
        while len(parts) > 1:
            parts = [parts[k] + parts[k + 1] for k in range(0, len(parts), 2)]
        return parts[0]

    def sum_over(x, bits, order=lambda got, mask: got, cross=None):
        for masks in rounds(bits):
            got = [
                swap(x, size, crossing(m, core) if cross is None else m ^ (core if cross >> (k + 1) & 1 else 0))
                for k, m in enumerate(masks)
            ]
            exact = total([x] + [order(g, m) for g, m in zip(got, masks)])
            x = exact.astype(jnp.bfloat16)
        return exact

    def per_device(passages, enc_weight, enc_bias, dec_weight, dec_bias, active):
        rows, width = passages.shape
        half = width // 2
        me = lax.axis_index(AXES)
        mine = lax.axis_index("sub")
        odd = me & (CROSS | core)
        for k in (16, 8, 4, 2, 1):
            odd = odd ^ (odd >> k)
        high = (odd & 1) == 1

        blocks = [passages] + [swap(passages, size, k ^ (core if FIRST >> k & 1 else 0)) for k in range(1, sub)]
        every = jnp.concatenate(blocks, axis=0)
        gate = jnp.concatenate(
            [lax.dynamic_slice_in_dim(active, (mine ^ k) * rows, rows, 0) for k in range(sub)], axis=0
        ).astype(jnp.float32)

        def join(own, other):
            left = jnp.where(high, other, own)
            right = jnp.where(high, own, other)
            return jnp.concatenate([left, right], axis=1)

        def reorder(got, mask):
            parts = [got[(k ^ mask) * rows : ((k ^ mask) + 1) * rows] for k in range(sub)]
            return jnp.concatenate(parts, axis=0)

        pre = jnp.concatenate(
            [
                jnp.dot(passages, enc_weight, preferred_element_type=jnp.float32),
                jnp.dot(every[rows:], enc_weight, preferred_element_type=jnp.float32),
            ],
            axis=0,
        )
        pre = pre + enc_bias
        codes = (gate * pre).astype(jnp.bfloat16)
        mine_at = jnp.where(high, half, 0)
        send = jnp.dot(
            codes,
            lax.dynamic_slice_in_dim(dec_weight, half - mine_at, half, 1),
            preferred_element_type=jnp.float32,
        ).astype(jnp.bfloat16)
        got = swap(send, size, core)
        keep = jnp.dot(
            codes,
            lax.dynamic_slice_in_dim(dec_weight, mine_at, half, 1),
            preferred_element_type=jnp.float32,
        )
        x = (lax.optimization_barrier(keep) + got.astype(jnp.float32)).astype(jnp.bfloat16)
        x = sum_over(x, sub_bits, reorder).astype(jnp.bfloat16)
        recon = sum_over(x, z_bits)
        base = dec_bias - every.astype(jnp.float32)
        own = (recon + jnp.where(high, base[:, half:], base[:, :half])).astype(jnp.bfloat16)
        other = swap(own, size, core)
        resid = join(own, other)
        mine_at = jnp.where(high, half, 0)

        dec_other = swap(dec_weight, size, core)
        gate_other = swap(gate.astype(jnp.bfloat16), size, core)

        def against(part, by, at):
            return lax.dot_general(
                part,
                lax.dynamic_slice_in_dim(by, at, half, 1),
                (((1,), (1,)), ((), ())),
                preferred_element_type=jnp.float32,
            )

        back = lax.optimization_barrier(against(own, dec_weight, mine_at))
        back_other = lax.optimization_barrier(against(own, dec_other, mine_at))
        back = back + against(other, dec_weight, half - mine_at)
        back_other = back_other + against(other, dec_other, half - mine_at)
        dpre = (gate * back).astype(jnp.bfloat16)
        dpre_other = lax.optimization_barrier(
            (gate_other.astype(jnp.float32) * back_other).astype(jnp.bfloat16)
        )
        weight = swap(enc_weight, size, core)

        def spread(part, by):
            return lax.dot_general(
                part, by, (((1,), (1,)), ((), ())), preferred_element_type=jnp.float32
            )

        grad = lax.optimization_barrier(spread(dpre, enc_weight))
        x = (grad + spread(dpre_other, weight)).astype(jnp.bfloat16)
        grad_dec = lax.dot_general(
            codes, resid, (((0,), (0,)), ((), ())), preferred_element_type=jnp.float32
        ).astype(jnp.bfloat16)
        grad_enc = lax.dot_general(
            every, dpre, (((0,), (0,)), ((), ())), preferred_element_type=jnp.float32
        ).astype(jnp.bfloat16)
        grad_dec_bias = jnp.sum(lax.optimization_barrier(resid).astype(jnp.float32), axis=0)
        grad_enc_bias = jnp.sum(lax.optimization_barrier(dpre).astype(jnp.float32), axis=0)

        got = [swap(x[k * rows : (k + 1) * rows], size, k ^ (core if OWN >> k & 1 else 0)) for k in range(1, sub)]
        x = total([x[:rows]] + got).astype(jnp.bfloat16)
        grad_input = sum_over(x, z_bits, cross=LAST) - resid[:rows].astype(jnp.float32)
        return (grad_enc, grad_enc_bias, grad_dec, grad_dec_bias, grad_input)

    return per_device


def solution(mesh):
    in_specs = (
        P("sub", None),
        P(None, ("wide", "sub")),
        P(("wide", "sub")),
        P(("wide", "sub"), None),
        P(),
        P(None, ("wide", "sub")),
    )
    out_specs = (
        P(None, ("wide", "sub")),
        P(("wide", "sub")),
        P(("wide", "sub"), None),
        P(),
        P("sub", None),
    )
    per_device = make_per_device(mesh.shape["wide"], mesh.shape["sub"])

    return jax.shard_map(per_device, mesh=mesh, in_specs=in_specs, out_specs=out_specs, check_vma=False)
```
